256 devices in a mesh: dp: 2 (over core), blk: 16 (over z, x_hi), head: 8 (over x_lo, y).
Axes of the slice: x: 4 (x_hi: 2, x_lo: 2; x = x_hi * 2 + x_lo), y: 4, z: 8, core: 2. Of those that a mesh axis runs over, the one named last changes fastest.
Arguments:
- queries: bfloat16 [16384, 5120], P(('dp', 'blk'), 'head'), parts along dimension 0, may hold values from -20 to 20, as said below
- keys: bfloat16 [16384, 5120], P(('dp', 'blk'), 'head'), parts along dimension 0, may hold values from -20 to 20
- values: bfloat16 [16384, 5120], P(('dp', 'blk'), 'head'), parts along dimension 0, may hold values from -6 to 6
- block_list: int32 [128, 16], P(('dp', 'blk')), parts along dimension 0, may hold values from 0 to 63, as said below
- block_count: int32 [128], P(('dp', 'blk')), parts along dimension 0, may hold values from 4 to 16, as said below
- out_weight: bfloat16 [5120, 5120], P('head'), may hold values from -0.25 to 0.25
Outputs:
- projected: bfloat16 [16384, 5120], P(('dp', 'blk', 'head')), parts along dimension 0
The draws below stay inside these ranges and needn't reach their ends.
There are 2 independent parts, one for each index of `dp`. The reference program is written for one: setup_inputs(seed, part) draws one part's arguments, and reference() takes and returns one part's arrays. A program takes and returns all parts, laid end to end along the dimension named above; an argument that names none is the same for every part. Nothing has to cross between parts.
Inputs may be any that keep to these rules, and one draw needn't show every extreme that they name: `block_list`: each row names 16 different key blocks of the same clip; its first entry is the query block itself; only the first block_count entries of a row are used. `block_count`: some query block uses all 16 entries in every draw. `queries`: query entries lie in the stated range.
All inputs are finite; a program needn't handle non-finite values.
Results may differ from the reference program's by a relative error of at most 0.02.
Values may be sent and summed in bfloat16 or wider, within the bound.
No kernel may reach another device: no remote copies, remote signals or barrier semaphores. Data moves between devices by JAX's collectives and lax.ppermute only.
A program may use at most 128 MiB of HBM per device.

```python
import math
import jax
import jax.numpy as jnp
from jax import lax

HEADS = 40
HD = 128
BS = 128
KB = 16
D = 5120
SEQ = 8192
NBLK = 64
N_HEAD = 8


def paired_fields(key):
    folded = jax.random.fold_in(key, 17)
    key_query, key_key = jax.random.split(folded, 2)
    query_part = 1.5 * jnp.clip(jax.random.normal(key_query, (SEQ, D), jnp.float32), -4.0, 4.0)
    key_part = 1.5 * jnp.clip(jax.random.normal(key_key, (SEQ, D), jnp.float32), -4.0, 4.0)
    return (query_part, key_part)


def draw_queries(key, part):
    return paired_fields(key)[0].astype(jnp.bfloat16)


def draw_keys(key, part):
    return paired_fields(key)[1].astype(jnp.bfloat16)


def mask_tables(key):
    folded = jax.random.fold_in(key, 23)
    key_order, key_start, key_count = jax.random.split(folded, 3)
    blocks = jnp.arange(NBLK, dtype=jnp.int32)
    distance = jnp.abs(blocks[:, None] - blocks[None, :])
    ranking = jax.random.randint(key_order, (NBLK, NBLK), 0, 65536, dtype=jnp.int32)
    ranking = ranking + jnp.where(distance == 1, 32768, 0) + jnp.where(distance == 0, 1048576, 0)
    ranking = ranking * NBLK + blocks[None, :]
    unused, lists = lax.top_k(ranking, KB)
    busy_start = jax.random.randint(key_start, (), 0, NBLK, dtype=jnp.int32)
    busy_blocks = (blocks - busy_start) % NBLK < max(NBLK // 4, 1)
    others = jax.random.randint(key_count, (NBLK,), max(KB // 4, 1), KB // 2 + 1, dtype=jnp.int32)
    counts = jnp.where(busy_blocks, KB, others)
    return (lists.astype(jnp.int32), counts.astype(jnp.int32))


def draw_block_list(key, part):
    return mask_tables(key)[0]


def draw_block_count(key, part):
    return mask_tables(key)[1]


def steps_of(stream_key, shape, shards, least, largest):
    def one(position, shards_of):
        heights = jax.random.uniform(jax.random.fold_in(jax.random.fold_in(stream_key, 6), position), (shards_of,), jnp.float32, least / len(shards), largest / len(shards))
        return jnp.repeat(jnp.exp(heights), shape[position] // shards_of).reshape((-1,) + (1,) * (len(shape) - position - 1))

    factor_of = one(*shards[0])
    for cut in shards[1:]:
        factor_of = factor_of * one(*cut)
    return factor_of


def gaussian(rng, dims, spread, limit, shards=(), held_as=jnp.bfloat16):
    loudness = steps_of(rng, dims, shards, -0.22, 0.18) if shards else 1.0
    result = jax.random.normal(rng, dims, jnp.float32) * spread * loudness
    return jnp.minimum(jnp.maximum(result, -limit), limit).astype(held_as)


def setup_inputs(seed: int = 0, part: int = 0) -> dict:
    splits = jax.random.split(jax.random.key(seed), 7)
    part_splits = jax.random.split(jax.random.fold_in(splits[6], part), 7)
    queries = draw_queries(jax.random.fold_in(jax.random.fold_in(splits[6], part), 71), part)
    keys = draw_keys(jax.random.fold_in(jax.random.fold_in(splits[6], part), 71), part)
    values = gaussian(part_splits[2], (SEQ, D), 1.0, 6.0, ((0, 16), (1, 8)))
    block_list = draw_block_list(jax.random.fold_in(jax.random.fold_in(splits[6], part), 71), part)
    block_count = draw_block_count(jax.random.fold_in(jax.random.fold_in(splits[6], part), 71), part)
    out_weight = gaussian(splits[5], (D, D), (D // 8) ** -0.5, 0.25, ((0, 8),))
    return dict(queries=queries, keys=keys, values=values, block_list=block_list, block_count=block_count, out_weight=out_weight)


def attend_block(block_index, query_grid, key_grid, value_grid, block_list, block_count):
    chosen = block_list[block_index].astype(jnp.int32)
    key_rows = key_grid[chosen].reshape(KB * BS, HEADS, HD).astype(jnp.float32)
    value_rows = value_grid[chosen].reshape(KB * BS, HEADS, HD).astype(jnp.float32)
    usable = jnp.repeat(jnp.arange(KB, dtype=jnp.int32) < block_count[block_index], BS)
    query_rows = query_grid[block_index].astype(jnp.float32)
    scores = jnp.einsum('qhd,khd->hqk', query_rows, key_rows) * (1.0 / math.sqrt(HD))
    scores = jnp.where(usable[None, None, :], scores, -jnp.inf)
    highest = lax.optimization_barrier(jnp.max(scores, axis=-1, keepdims=True))
    weights = jnp.where(usable[None, None, :], jnp.exp(scores - highest), 0.0)
    totals = lax.optimization_barrier(jnp.sum(weights, axis=-1))
    rounded = lax.optimization_barrier(weights.astype(jnp.bfloat16)).astype(jnp.float32)
    mixed = jnp.einsum('hqk,khd->qhd', rounded, value_rows)
    return (mixed / jnp.transpose(totals)[:, :, None]).astype(jnp.bfloat16).reshape(BS, D)

def reference(queries, keys, values, block_list, block_count, out_weight):
    query_grid = queries.reshape(NBLK, BS, HEADS, HD)
    key_grid = keys.reshape(NBLK, BS, HEADS, HD)
    value_grid = values.reshape(NBLK, BS, HEADS, HD)

    def one_block(block_index):
        return attend_block(block_index, query_grid, key_grid, value_grid, block_list, block_count)
    attended = lax.map(one_block, jnp.arange(NBLK, dtype=jnp.int32)).reshape(SEQ, D)
    group_width = D // N_HEAD
    combined = jnp.zeros((SEQ, D), jnp.float32)
    for group in range(N_HEAD):
        part_in = attended[:, group * group_width:(group + 1) * group_width]
        part_weight = out_weight[group * group_width:(group + 1) * group_width, :]
        partial_sum = jnp.dot(part_in, part_weight, preferred_element_type=jnp.float32)
        rounded_sum = lax.optimization_barrier(partial_sum.astype(jnp.bfloat16)).astype(jnp.float32)
        combined = combined + rounded_sum
    return combined.astype(jnp.bfloat16)
```

```python
import math

import jax
import jax.numpy as jnp
from jax import lax
from jax.experimental import pallas as pl
from jax.experimental.pallas import tpu as pltpu
from jax.sharding import PartitionSpec as P

HD = 128
BS = 128
KB = 16
TAB = 16
GROUP = 4
NZ = 8
NX = 2
NY = 4
LEVELS = ((0, 2, 3, 5, 6), (1, 3, 4, 6, 7))
SERVED = tuple(tuple(lv.index(z) if z in lv else -1 for z in range(NZ)) for lv in LEVELS)
BOTH = ("blk", "head")


def flat(z, xh, head):
    return (z * NX + xh) * 2 * NY + head


def pairs(shift):
    out = []
    for head in range(2 * NY):
        for z in range(NZ):
            to = (z + shift) % NZ
            if SERVED[head // NY][to] >= 0:
                for xh in range(NX):
                    out.append((flat(z, xh, head), flat(to, xh, head)))
    return out


def swap_pairs():
    out = []
    for head in range(2 * NY):
        for z in LEVELS[head // NY]:
            for xh in range(NX):
                out.append((flat(z, xh, head), flat(z, 1 - xh, head)))
    return out


def attend_kernel(lists, counts, *refs):
    own = refs[:NZ]
    other = refs[NZ : 2 * NZ]
    out = refs[2 * NZ]
    kbuf, vbuf, qbuf, sbuf, sems = refs[2 * NZ + 1 :]
    rows = out.shape[0] // NZ
    factor = math.log2(math.e) / math.sqrt(HD)

    copies = []
    for s in range(NZ):
        for src, dst, i in (
            (own[s].at[pl.ds(0 * rows, rows)], kbuf.at[pl.ds(s * rows, rows)], 0),
            (own[s].at[pl.ds(1 * rows, rows)], vbuf.at[pl.ds(s * rows, rows)], 1),
            (own[s].at[pl.ds(2 * rows, rows)], qbuf.at[pl.ds(s * rows, rows)], 2),
            (other[s].at[pl.ds(0 * rows, rows)], kbuf.at[pl.ds((NZ + s) * rows, rows)], 3),
            (other[s].at[pl.ds(1 * rows, rows)], vbuf.at[pl.ds((NZ + s) * rows, rows)], 4),
        ):
            copies.append(pltpu.make_async_copy(src, dst, sems.at[s, i]))
    for c in copies:
        c.start()
    for c in copies:
        c.wait()

    def gather(buf, qb, g):
        parts = []
        for j in range(GROUP):
            at = pl.multiple_of(lists[qb * KB + g * GROUP + j] * BS, BS)
            parts.append(buf[pl.ds(at, BS), :])
        return jnp.concatenate(parts, axis=0)

    def branch(qb, n, groups):
        q = qbuf[pl.ds(pl.multiple_of(qb * BS, BS), BS), :]
        high = None
        for g in range(groups):
            s = lax.dot_general(
                q, gather(kbuf, qb, g), (((1,), (1,)), ((), ())), preferred_element_type=jnp.float32
            )
            if g == groups - 1:
                lane = lax.broadcasted_iota(jnp.int32, s.shape, 1)
                s = jnp.where(lane < (n - g * GROUP) * BS, s, -1e30)
            sbuf[:, g * GROUP * BS : (g + 1) * GROUP * BS] = s
            for j in range(GROUP):
                t = s[:, j * BS : (j + 1) * BS]
                high = t if high is None else jnp.maximum(high, t)
        m = jnp.max(high, axis=-1, keepdims=True)
        acc = None
        tot = None
        for g in range(groups):
            p = jnp.exp2((sbuf[:, g * GROUP * BS : (g + 1) * GROUP * BS] - m) * factor)
            for j in range(GROUP):
                t = p[:, j * BS : (j + 1) * BS]
                tot = t if tot is None else tot + t
            part = jnp.dot(
                p.astype(jnp.bfloat16), gather(vbuf, qb, g), preferred_element_type=jnp.float32
            )
            acc = part if acc is None else acc + part
        total = jnp.sum(tot, axis=-1, keepdims=True)
        out[pl.ds(pl.multiple_of(qb * BS, BS), BS), :] = (acc / total).astype(out.dtype)

    def step(qb, carry):
        n = counts[qb]
        for groups in range(1, KB // GROUP + 1):

            @pl.when((n > (groups - 1) * GROUP) & (n <= groups * GROUP))
            def _():
                branch(qb, n, groups)

        return carry

    lax.fori_loop(0, out.shape[0] // BS, step, 0)


def attend(lists, counts, own, other, rows):
    any_spec = pl.BlockSpec(memory_space=pl.ANY)
    smem = pl.BlockSpec(memory_space=pltpu.SMEM)
    return pl.pallas_call(
        attend_kernel,
        out_shape=jax.ShapeDtypeStruct((NZ * rows, HD), jnp.bfloat16),
        in_specs=[smem, smem] + [any_spec] * (2 * NZ),
        out_specs=pl.BlockSpec(memory_space=pltpu.VMEM),
        scratch_shapes=[
            pltpu.VMEM((2 * NZ * rows, HD), jnp.bfloat16),
            pltpu.VMEM((2 * NZ * rows, HD), jnp.bfloat16),
            pltpu.VMEM((NZ * rows, HD), jnp.bfloat16),
            pltpu.VMEM((BS, KB * BS), jnp.float32),
            pltpu.SemaphoreType.DMA((NZ, 5)),
        ],
        compiler_params=pltpu.CompilerParams(vmem_limit_bytes=24 << 20),
        cost_estimate=pl.CostEstimate(
            flops=32 * 8 * 4 * BS * BS * HD, bytes_accessed=6 << 20, transcendentals=32 * 8 * BS * BS
        ),
        name="attend",
    )(lists, counts, *own, *other)


def on_device(queries, keys, values, block_list, block_count, out_weight):
    rows, width = queries.shape
    heads = width // HD
    blk, head = lax.axis_index("blk"), lax.axis_index("head")
    z, xh, x_lo = blk // NX, blk % NX, head // NY
    served = jnp.asarray(SERVED, jnp.int32)[x_lo]
    levels = jnp.asarray(LEVELS, jnp.int32)[x_lo]

    table = jnp.concatenate([block_list, block_count[:, None]], axis=1).astype(jnp.bfloat16)
    table = jnp.pad(table, ((0, TAB - table.shape[0]), (0, HD - table.shape[1])))

    def payload(shift):
        at = jnp.maximum(served[(z + shift) % NZ], 0) * HD
        return jnp.concatenate(
            [lax.dynamic_slice_in_dim(a, at, HD, 1) for a in (keys, values, queries)] + [table]
        )

    own = [None] * NZ
    other = [None] * NZ
    swap = swap_pairs()
    for s in (0, 4, 3, 5, 2, 6, 1, 7):
        sent = payload(s)
        own[s] = sent if s == 0 else lax.ppermute(sent, BOTH, pairs(s))
    for s in (0, 4, 3, 5, 2, 6, 1, 7):
        other[s] = lax.ppermute(own[s][: 2 * rows], BOTH, swap)

    per = rows // BS
    table = jnp.stack([o[3 * rows : 3 * rows + per, : KB + 1] for o in own]).astype(jnp.int32)
    kblk = table[..., :KB] // per
    slot = (z - kblk // NX) % NZ + jnp.where(kblk % NX == xh, 0, NZ)
    lists = (slot * per + table[..., :KB] % per).reshape(-1)
    counts = jnp.where(served[z] >= 0, table[..., KB].reshape(-1), 0)

    mixed = attend(lists, counts, own, other, rows)
    back = []
    for s in range(NZ):
        piece = mixed[s * rows : (s + 1) * rows]
        if s:
            piece = lax.ppermute(piece, BOTH, [(b, a) for a, b in pairs(s)])
        back.append(piece)
    back = jnp.stack(back)
    attended = jnp.concatenate(
        [lax.dynamic_index_in_dim(back, (levels[h] - z) % NZ, 0, False) for h in range(heads)], axis=1
    )
    return lax.psum_scatter(
        jnp.dot(attended, out_weight, preferred_element_type=jnp.float32).astype(jnp.bfloat16),
        "head",
        scatter_dimension=0,
        tiled=True,
    )


def solution(mesh):
    placed = (
        P(("dp", "blk"), "head"),
        P(("dp", "blk"), "head"),
        P(("dp", "blk"), "head"),
        P(("dp", "blk"), None),
        P(("dp", "blk")),
        P("head", None),
    )
    return jax.shard_map(
        on_device,
        mesh=mesh,
        in_specs=placed,
        out_specs=P(("dp", "blk", "head"), None),
        check_vma=False,
    )
```

```python
import functools
import math

import jax
import jax.numpy as jnp
from jax import lax
from jax.experimental import pallas as pl
from jax.experimental.pallas import tpu as pltpu
from jax.sharding import PartitionSpec as P

HD = 128
BS = 128
KB = 16
TAB = 16
FIRST = 1536
NZ = 8
NX = 2
NY = 4
FIRST = 1536
LOW = -1e30
FACTOR = math.log2(math.e) / math.sqrt(HD)


def attend_kernel(chunks, first, last, base, flags, q, *refs):
    keys, values = refs[:chunks], refs[chunks : 2 * chunks]
    refs = refs[2 * chunks :]
    heads = q.shape[1] // HD
    per = keys[0].shape[0] // BS
    if first:
        mixed, stats = refs
    else:
        mixed_in, stats_in, mixed, stats = refs[:4]
    acc = refs[4] if last else mixed
    tiles = acc.shape[0]
    if first:
        acc[...] = jnp.zeros_like(acc)
        row = lax.broadcasted_iota(jnp.int32, stats.shape, 1)
        stats[...] = jnp.where(row == 0, LOW, 0.0)
    else:
        acc[...] = mixed_in[base : base + tiles]
        stats[...] = stats_in[base : base + tiles]

    def visit(qb, c, j):
        at = pl.ds(pl.multiple_of(j * BS, BS), BS)
        rows = pl.ds(pl.multiple_of((qb + base // heads) * BS, BS), BS)
        cols = [slice(h * HD, (h + 1) * HD) for h in range(heads)]
        before = [stats[qb * heads + h] for h in range(heads)]
        held = [acc[qb * heads + h] for h in range(heads)]
        scores = [
            lax.dot_general(
                keys[c][at, col], q[rows, col], (((1,), (1,)), ((), ())), preferred_element_type=jnp.float32
            )
            for col in cols
        ]
        after_it = []
        for h in range(heads):
            old, tot = before[h][0:1], before[h][1:2]
            new = jnp.maximum(old, jnp.max(scores[h], axis=0, keepdims=True))
            p = jnp.exp2((scores[h] - new) * FACTOR)
            scale = jnp.exp2((old - new) * FACTOR)
            tot = tot * scale + jnp.sum(p, axis=0, keepdims=True)
            add = lax.dot_general(
                values[c][at, cols[h]],
                p.astype(jnp.bfloat16),
                (((0,), (0,)), ((), ())),
                preferred_element_type=jnp.float32,
            )
            after_it.append((new, tot, held[h] * scale + add))
        for h in range(heads):
            new, tot, total = after_it[h]
            stats[qb * heads + h, 0:1] = new
            stats[qb * heads + h, 1:2] = tot
            acc[qb * heads + h] = total

    def step(n, carry):
        qb, j = n // per, n % per
        for c in range(chunks):

            @pl.when(flags[c, qb + base // heads, j] > 0)
            def _():
                visit(qb, c, j)

        return carry

    lax.fori_loop(0, tiles // heads * per, step, 0)
    if last and base:
        mixed[...] = acc[...].astype(mixed.dtype)
    elif last:
        mixed[...] = acc[...]


def attend(flags, q, keys, values, state, part):
    vmem = pl.BlockSpec(memory_space=pltpu.VMEM)
    smem = pl.BlockSpec(memory_space=pltpu.SMEM)
    last = part is not None
    tiles = q.shape[0] // BS * (q.shape[1] // HD) // (2 if last else 1)
    chunks = len(keys)
    first = state is None
    state = () if first else state
    at = 2 + 2 * chunks
    shape = (tiles, HD, BS)
    return pl.pallas_call(
        functools.partial(attend_kernel, chunks, first, last, tiles * (part or 0)),
        out_shape=(
            jax.ShapeDtypeStruct(shape, jnp.bfloat16 if part else jnp.float32),
            jax.ShapeDtypeStruct((tiles, 8, BS), jnp.float32),
        ),
        in_specs=[smem] + [vmem] * (1 + 2 * chunks + len(state)),
        out_specs=(vmem, vmem),
        input_output_aliases={} if first or last else {at: 0, at + 1: 1},
        scratch_shapes=[pltpu.VMEM(shape, jnp.float32)] if last else [],
        compiler_params=pltpu.CompilerParams(vmem_limit_bytes=24 << 20),
        cost_estimate=pl.CostEstimate(
            flops=tiles * chunks * 100000000, bytes_accessed=4 << 20, transcendentals=chunks << 20
        ),
        name="attend",
    )(flags, q, *keys, *values, *state)


def finish_kernel(mixed, stats, mixed_other, stats_other, out):
    heads = out.shape[1] // HD
    for i in range(mixed.shape[0]):
        m0, l0 = stats[i, 0:1], stats[i, 1:2]
        m1, l1 = stats_other[i, 0:1], stats_other[i, 1:2]
        m = jnp.maximum(m0, m1)
        a0 = jnp.exp2((m0 - m) * FACTOR)
        a1 = jnp.exp2((m1 - m) * FACTOR)
        total = l0 * a0 + l1 * a1
        both = mixed[i] * (a0 / total) + mixed_other[i].astype(jnp.float32) * (a1 / total)
        qb, h = i // heads, i % heads
        out[qb * BS : (qb + 1) * BS, h * HD : (h + 1) * HD] = both.T.astype(out.dtype)


def finish(own, other, shape):
    vmem = pl.BlockSpec(memory_space=pltpu.VMEM)
    return pl.pallas_call(
        finish_kernel,
        out_shape=jax.ShapeDtypeStruct(shape, jnp.bfloat16),
        in_specs=[vmem] * 4,
        out_specs=vmem,
        compiler_params=pltpu.CompilerParams(vmem_limit_bytes=16 << 20),
        cost_estimate=pl.CostEstimate(flops=2000000000, bytes_accessed=4 << 20, transcendentals=1 << 10),
        name="finish",
    )(*own, *other)


def after(x, *behind):
    return lax.optimization_barrier((x,) + behind)[0] if behind else x


def project(attended, weight, head):
    x, y = head // NY, head % NY
    rows = attended.shape[0] // (2 * NY)
    width = weight.shape[1]
    tiles = attended.reshape(2, NY, rows, -1)
    other_x = [(h, (h + NY) % (2 * NY)) for h in range(2 * NY)]

    def part(a, lo, hi):
        return jnp.dot(a, weight[:, lo:hi], preferred_element_type=jnp.float32)

    def narrow(a):
        return a.astype(jnp.bfloat16)

    def wide(a):
        return a.astype(jnp.float32)

    def ring(term, way):
        perm = [(h, h // NY * NY + (h % NY + way) % NY) for h in range(2 * NY)]
        acc = narrow(term((y - way) % NY))
        for s in range(NY - 1):
            acc = lax.ppermute(acc, "head", perm)
            acc = narrow(wide(acc) + term((y - way * (s + 2)) % NY))
        return acc

    cut = FIRST
    mid = cut + (width - cut) // 2
    far = lax.dynamic_index_in_dim(tiles, 1 - x, 0, False).reshape(NY * rows, -1)
    near = lax.dynamic_index_in_dim(tiles, x, 0, False).reshape(NY * rows, -1)
    got = lax.ppermute(narrow(part(far, 0, cut)), "head", other_x)

    def both(i):
        return lax.dynamic_index_in_dim(tiles, i, 1, False).reshape(2 * rows, -1)

    up = ring(lambda i: part(both(i), cut, mid), 1)
    down = ring(lambda i: part(both(i), mid, width), -1)
    half = narrow(wide(got) + part(near, 0, cut)).reshape(NY, rows, cut)
    left = ring(lambda i: wide(lax.dynamic_index_in_dim(half[..., : cut // 2], i, 0, False)), 1)
    right = ring(lambda i: wide(lax.dynamic_index_in_dim(half[..., cut // 2 :], i, 0, False)), -1)
    late = jnp.concatenate([up, down], axis=1).reshape(2, rows, width - cut)
    give = lax.ppermute(lax.dynamic_index_in_dim(late, 1 - x, 0, False), "head", other_x)
    keep = lax.dynamic_index_in_dim(late, x, 0, False)
    return jnp.concatenate([left, right, narrow(wide(give) + wide(keep))], axis=1)


def on_device(queries, keys, values, block_list, block_count, out_weight):
    rows, width = queries.shape
    per = rows // BS
    blk, head = lax.axis_index("blk"), lax.axis_index("head")
    z, xh = blk // NX, blk % NX
    cross = [(b, b ^ 1) for b in range(NZ * NX)]
    up = [(b, (b + NX) % (NZ * NX)) for b in range(NZ * NX)]
    down = [(b, a) for a, b in up]

    asked = lax.ppermute(jnp.concatenate([block_list, block_count[:, None]], axis=1), "blk", cross)
    both = jnp.concatenate([queries, lax.ppermute(queries, "blk", cross)])
    table = jnp.stack([jnp.concatenate([block_list, block_count[:, None]], axis=1), asked])
    listed = jnp.arange(KB, dtype=jnp.int32) < table[..., KB:]
    seen = jnp.any(
        listed[..., None] & (table[..., :KB, None] == jnp.arange(NZ * NX * per, dtype=jnp.int32)), axis=2
    ).astype(jnp.int32)
    seen = lax.dynamic_index_in_dim(seen.reshape(2 * per, NZ, NX, per), xh, 2, False)
    flags = jnp.transpose(seen, (1, 0, 2))[(z - jnp.arange(NZ)) % NZ]

    def visit(stage, state, part=None):
        return attend(
            jnp.stack([flags[d] for d, _, _ in stage]),
            both,
            [k for _, k, _ in stage],
            [v for _, _, v in stage],
            state,
            part,
        )

    stage = ((0, keys, values),)
    state = None
    ups, downs = (keys, values), (keys, values)
    for s in range(1, NZ // 2 + 1):
        if s < NZ // 2:
            ups = tuple(lax.ppermute(a, "blk", up) for a in ups)
            downs = tuple(lax.ppermute(a, "blk", down) for a in downs)
            coming = ((s, *ups), (NZ - s, *downs))
        else:
            coming = ((s, lax.ppermute(ups[0], "blk", up), lax.ppermute(downs[1], "blk", down)),)
        state = visit(stage, state)
        if s < NZ // 2:
            ups = tuple(after(a, state[1]) for a in ups)
            downs = tuple(after(a, state[1]) for a in downs)
        stage = coming
    theirs = visit(stage, state, 1)
    other = [lax.ppermute(a, "blk", cross) for a in theirs]
    mine = visit(stage, state, 0)
    attended = finish(mine, other, (rows, width))
    return project(attended, out_weight, head)


def solution(mesh):
    placed = (
        P(("dp", "blk"), "head"),
        P(("dp", "blk"), "head"),
        P(("dp", "blk"), "head"),
        P(("dp", "blk"), None),
        P(("dp", "blk")),
        P("head", None),
    )
    return jax.shard_map(
        on_device,
        mesh=mesh,
        in_specs=placed,
        out_specs=P(("dp", "blk", "head"), None),
        check_vma=False,
    )
```

```python
import functools
import math

import jax
import jax.numpy as jnp
from jax import lax
from jax.experimental import pallas as pl
from jax.experimental.pallas import tpu as pltpu
from jax.sharding import PartitionSpec as P

HD = 128
BS = 128
KB = 16
TAB = 16
NZ = 8
NX = 2
NY = 4
LOW = -1e30
FACTOR = math.log2(math.e) / math.sqrt(HD)


def attend_kernel(chunks, first, last, base, flags, q, *refs):
    keys, values = refs[:chunks], refs[chunks : 2 * chunks]
    refs = refs[2 * chunks :]
    heads = q.shape[1] // HD
    per = keys[0].shape[0] // BS
    if first:
        mixed, stats = refs
    else:
        mixed_in, stats_in, mixed, stats = refs[:4]
    acc = refs[4] if last else mixed
    tiles = acc.shape[0]
    if first:
        acc[...] = jnp.zeros_like(acc)
        row = lax.broadcasted_iota(jnp.int32, stats.shape, 1)
        stats[...] = jnp.where(row == 0, LOW, 0.0)
    else:
        acc[...] = mixed_in[base : base + tiles]
        stats[...] = stats_in[base : base + tiles]

    def visit(qb, c, j):
        at = pl.ds(pl.multiple_of(j * BS, BS), BS)
        rows = pl.ds(pl.multiple_of((qb + base // heads) * BS, BS), BS)
        cols = [slice(h * HD, (h + 1) * HD) for h in range(heads)]
        before = [stats[qb * heads + h] for h in range(heads)]
        held = [acc[qb * heads + h] for h in range(heads)]
        scores = [
            lax.dot_general(
                keys[c][at, col], q[rows, col], (((1,), (1,)), ((), ())), preferred_element_type=jnp.float32
            )
            for col in cols
        ]
        after_it = []
        for h in range(heads):
            old, tot = before[h][0:1], before[h][1:2]
            new = jnp.maximum(old, jnp.max(scores[h], axis=0, keepdims=True))
            p = jnp.exp2((scores[h] - new) * FACTOR)
            scale = jnp.exp2((old - new) * FACTOR)
            tot = tot * scale + jnp.sum(p, axis=0, keepdims=True)
            add = lax.dot_general(
                values[c][at, cols[h]],
                p.astype(jnp.bfloat16),
                (((0,), (0,)), ((), ())),
                preferred_element_type=jnp.float32,
            )
            after_it.append((new, tot, held[h] * scale + add))
        for h in range(heads):
            new, tot, total = after_it[h]
            stats[qb * heads + h, 0:1] = new
            stats[qb * heads + h, 1:2] = tot
            acc[qb * heads + h] = total

    def step(n, carry):
        qb, j = n // per, n % per
        for c in range(chunks):

            @pl.when(flags[c, qb + base // heads, j] > 0)
            def _():
                visit(qb, c, j)

        return carry

    lax.fori_loop(0, tiles // heads * per, step, 0)
    if last and base:
        mixed[...] = acc[...].astype(mixed.dtype)
    elif last:
        mixed[...] = acc[...]


def attend(flags, q, keys, values, state, part):
    vmem = pl.BlockSpec(memory_space=pltpu.VMEM)
    smem = pl.BlockSpec(memory_space=pltpu.SMEM)
    last = part is not None
    tiles = q.shape[0] // BS * (q.shape[1] // HD) // (2 if last else 1)
    chunks = len(keys)
    first = state is None
    state = () if first else state
    at = 2 + 2 * chunks
    shape = (tiles, HD, BS)
    return pl.pallas_call(
        functools.partial(attend_kernel, chunks, first, last, tiles * (part or 0)),
        out_shape=(
            jax.ShapeDtypeStruct(shape, jnp.bfloat16 if part else jnp.float32),
            jax.ShapeDtypeStruct((tiles, 8, BS), jnp.float32),
        ),
        in_specs=[smem] + [vmem] * (1 + 2 * chunks + len(state)),
        out_specs=(vmem, vmem),
        input_output_aliases={} if first or last else {at: 0, at + 1: 1},
        scratch_shapes=[pltpu.VMEM(shape, jnp.float32)] if last else [],
        compiler_params=pltpu.CompilerParams(vmem_limit_bytes=24 << 20),
        cost_estimate=pl.CostEstimate(
            flops=tiles * chunks * 100000000, bytes_accessed=4 << 20, transcendentals=chunks << 20
        ),
        name="attend",
    )(flags, q, *keys, *values, *state)


def finish_kernel(mixed, stats, mixed_other, stats_other, out):
    heads, rows = out.shape[3] // HD, out.shape[2]
    for i in range(mixed.shape[0]):
        m0, l0 = stats[i, 0:1], stats[i, 1:2]
        m1, l1 = stats_other[i, 0:1], stats_other[i, 1:2]
        m = jnp.maximum(m0, m1)
        a0 = jnp.exp2((m0 - m) * FACTOR)
        a1 = jnp.exp2((m1 - m) * FACTOR)
        total = l0 * a0 + l1 * a1
        both = mixed[i] * (a0 / total) + mixed_other[i].astype(jnp.float32) * (a1 / total)
        qb, h = i // heads, i % heads
        done = both.T.astype(out.dtype)
        for t in range(BS // rows):
            x, y = divmod(qb * (BS // rows) + t, NY)
            out[x, y, :, h * HD : (h + 1) * HD] = done[t * rows : (t + 1) * rows]


def finish(own, other, shape):
    vmem = pl.BlockSpec(memory_space=pltpu.VMEM)
    return pl.pallas_call(
        finish_kernel,
        out_shape=jax.ShapeDtypeStruct(shape, jnp.bfloat16),
        in_specs=[vmem] * 4,
        out_specs=vmem,
        compiler_params=pltpu.CompilerParams(vmem_limit_bytes=16 << 20),
        cost_estimate=pl.CostEstimate(flops=2000000000, bytes_accessed=4 << 20, transcendentals=1 << 10),
        name="finish",
    )(*own, *other)


def after(x, *behind):
    return lax.optimization_barrier((x,) + behind)[0] if behind else x


def over_x(a):
    return lax.ppermute(a, "head", [(h, (h + NY) % (2 * NY)) for h in range(2 * NY)])


def over_dp(a):
    return lax.ppermute(a, "dp", [(0, 1), (1, 0)])


def project(attended, weights, head, core):
    x, y = head // NY, head % NY

    def at(a, i):
        return lax.dynamic_index_in_dim(a, i % NY, 0, False)

    give = lax.dynamic_index_in_dim(attended, 1 - x, 0, False)
    keep = lax.dynamic_index_in_dim(attended, x, 0, False)
    order = (y - 1, y + 1, y + 2, y)
    got = [over_x(jnp.concatenate([at(give, i) for i in pair])) for pair in (order[:2], order[2:])]
    local = jnp.concatenate([at(keep, i) for i in order])

    rows = got[0].shape[0]
    base = [jnp.dot(local, pair[0], preferred_element_type=jnp.float32) for pair in weights]

    def terms(n, acts, half):
        part = jnp.dot(acts, weights[half][1], preferred_element_type=jnp.float32)
        return jnp.split(part + base[half][n * rows : (n + 1) * rows], 2)

    def narrow(a):
        return a.astype(jnp.bfloat16)

    def turn(a, way):
        to = [(h, h // NY * NY + (h % NY + way) % NY) for h in range(2 * NY)]
        return lax.ppermute(a, "head", to).astype(jnp.float32)

    before, ahead = terms(0, got[0], 0)
    before_down, ahead_down = terms(0, got[0], 1)
    up, down, late = lax.optimization_barrier((narrow(before), narrow(ahead_down), got[1]))
    over, own = terms(1, late, 0)
    over_down, own_down = terms(1, late, 1)
    up = narrow(turn(up, 1) + over)
    down = narrow(turn(down, -1) + over_down)
    for here, here_down in ((ahead, before_down), (own, own_down)):
        up = narrow(turn(up, 1) + here)
        down = narrow(turn(down, -1) + here_down)
    return jnp.where(core == 0, jnp.concatenate([up, down], axis=1), jnp.concatenate([down, up], axis=1))


def on_device(queries, keys, values, block_list, block_count, out_weight):
    rows, width = queries.shape
    per = rows // BS
    blk, head, core = lax.axis_index("blk"), lax.axis_index("head"), lax.axis_index("dp")
    z, xh = blk // NX, blk % NX
    cross = [(b, b ^ 1) for b in range(NZ * NX)]
    up = [(b, (b + NX) % (NZ * NX)) for b in range(NZ * NX)]
    down = [(b, a) for a, b in up]

    asked = lax.ppermute(jnp.concatenate([block_list, block_count[:, None]], axis=1), "blk", cross)
    both = jnp.concatenate([queries, lax.ppermute(queries, "blk", cross)])
    table = jnp.stack([jnp.concatenate([block_list, block_count[:, None]], axis=1), asked])
    listed = jnp.arange(KB, dtype=jnp.int32) < table[..., KB:]
    seen = jnp.any(
        listed[..., None] & (table[..., :KB, None] == jnp.arange(NZ * NX * per, dtype=jnp.int32)), axis=2
    ).astype(jnp.int32)
    seen = lax.dynamic_index_in_dim(seen.reshape(2 * per, NZ, NX, per), xh, 2, False)
    flags = jnp.transpose(seen, (1, 0, 2))[(z - jnp.arange(NZ)) % NZ]

    def visit(stage, state, part=None):
        return attend(
            jnp.stack([flags[d] for d, _, _ in stage]),
            both,
            [k for _, k, _ in stage],
            [v for _, _, v in stage],
            state,
            part,
        )

    stage = ((0, keys, values),)
    state = None
    ups, downs = (keys, values), (keys, values)
    for s in range(1, NZ // 2 + 1):
        if s < NZ // 2:
            ups = tuple(lax.ppermute(a, "blk", up) for a in ups)
            downs = tuple(lax.ppermute(a, "blk", down) for a in downs)
            coming = ((s, *ups), (NZ - s, *downs))
        else:
            coming = ((s, lax.ppermute(ups[0], "blk", up), lax.ppermute(downs[1], "blk", down)),)
        if s == 1:
            half = out_weight.shape[1] // 2
            held = after(out_weight, ups[0])
            ours = lax.dynamic_slice_in_dim(held, core * half, half, 1)
            rest = lax.dynamic_slice_in_dim(held, (1 - core) * half, half, 1)
            fetched = over_x(ours)
        state = visit(stage, state)
        if s < NZ // 2:
            ups = tuple(after(a, state[1]) for a in ups)
            downs = tuple(after(a, state[1]) for a in downs)
        stage = coming
    theirs = visit(stage, state, 1)
    other = [lax.ppermute(a, "blk", cross) for a in theirs]
    mine = visit(stage, state, 0)
    swapped = over_dp(after(fetched, state[1]))
    attended = finish(mine, other, (2, NY, rows // (2 * NY), width))
    return project(attended, ((ours, fetched), (rest, swapped)), head, core)


def solution(mesh):
    placed = (
        P(("dp", "blk"), "head"),
        P(("dp", "blk"), "head"),
        P(("dp", "blk"), "head"),
        P(("dp", "blk"), None),
        P(("dp", "blk")),
        P("head", None),
    )
    return jax.shard_map(
        on_device,
        mesh=mesh,
        in_specs=placed,
        out_specs=P(("dp", "blk", "head"), None),
        check_vma=False,
    )
```

```python
import functools
import math

import jax
import jax.numpy as jnp
from jax import lax
from jax.experimental import pallas as pl
from jax.experimental.pallas import tpu as pltpu
from jax.sharding import PartitionSpec as P

HD = 128
BS = 128
KB = 16
TAB = 16
NZ = 8
NX = 2
NY = 4
LOW = -1e30
FACTOR = math.log2(math.e) / math.sqrt(HD)


def attend_kernel(chunks, first, last, base, flags, q, *refs):
    keys, values = refs[:chunks], refs[chunks : 2 * chunks]
    refs = refs[2 * chunks :]
    heads = q.shape[1] // HD
    per = keys[0].shape[0] // BS
    if first:
        mixed, stats = refs
    else:
        mixed_in, stats_in, mixed, stats = refs[:4]
    acc = refs[4] if last else mixed
    tiles = acc.shape[0]
    if first:
        acc[...] = jnp.zeros_like(acc)
        row = lax.broadcasted_iota(jnp.int32, stats.shape, 1)
        stats[...] = jnp.where(row == 0, LOW, 0.0)
    else:
        acc[...] = mixed_in[base : base + tiles]
        stats[...] = stats_in[base : base + tiles]

    def visit(qb, c, j):
        at = pl.ds(pl.multiple_of(j * BS, BS), BS)
        rows = pl.ds(pl.multiple_of((qb + base // heads) * BS, BS), BS)
        cols = [slice(h * HD, (h + 1) * HD) for h in range(heads)]
        before = [stats[qb * heads + h] for h in range(heads)]
        held = [acc[qb * heads + h] for h in range(heads)]
        scores = [
            lax.dot_general(
                keys[c][at, col], q[rows, col], (((1,), (1,)), ((), ())), preferred_element_type=jnp.float32
            )
            for col in cols
        ]
        after_it = []
        for h in range(heads):
            old, tot = before[h][0:1], before[h][1:2]
            new = jnp.maximum(old, jnp.max(scores[h], axis=0, keepdims=True))
            p = jnp.exp2((scores[h] - new) * FACTOR)
            scale = jnp.exp2((old - new) * FACTOR)
            tot = tot * scale + jnp.sum(p, axis=0, keepdims=True)
            add = lax.dot_general(
                values[c][at, cols[h]],
                p.astype(jnp.bfloat16),
                (((0,), (0,)), ((), ())),
                preferred_element_type=jnp.float32,
            )
            after_it.append((new, tot, held[h] * scale + add))
        for h in range(heads):
            new, tot, total = after_it[h]
            stats[qb * heads + h, 0:1] = new
            stats[qb * heads + h, 1:2] = tot
            acc[qb * heads + h] = total

    def step(n, carry):
        qb, j = n // per, n % per
        for c in range(chunks):

            @pl.when(flags[c, qb + base // heads, j] > 0)
            def _():
                visit(qb, c, j)

        return carry

    lax.fori_loop(0, tiles // heads * per, step, 0)
    if last and base:
        mixed[...] = acc[...].astype(mixed.dtype)
    elif last:
        mixed[...] = acc[...]


def attend(flags, q, keys, values, state, part):
    vmem = pl.BlockSpec(memory_space=pltpu.VMEM)
    smem = pl.BlockSpec(memory_space=pltpu.SMEM)
    last = part is not None
    tiles = q.shape[0] // BS * (q.shape[1] // HD) // (2 if last else 1)
    chunks = len(keys)
    first = state is None
    state = () if first else state
    at = 2 + 2 * chunks
    shape = (tiles, HD, BS)
    return pl.pallas_call(
        functools.partial(attend_kernel, chunks, first, last, tiles * (part or 0)),
        out_shape=(
            jax.ShapeDtypeStruct(shape, jnp.bfloat16 if part else jnp.float32),
            jax.ShapeDtypeStruct((tiles, 8, BS), jnp.float32),
        ),
        in_specs=[smem] + [vmem] * (1 + 2 * chunks + len(state)),
        out_specs=(vmem, vmem),
        input_output_aliases={} if first or last else {at: 0, at + 1: 1},
        scratch_shapes=[pltpu.VMEM(shape, jnp.float32)] if last else [],
        compiler_params=pltpu.CompilerParams(vmem_limit_bytes=24 << 20),
        cost_estimate=pl.CostEstimate(
            flops=tiles * chunks * 100000000, bytes_accessed=4 << 20, transcendentals=chunks << 20
        ),
        name="attend",
    )(flags, q, *keys, *values, *state)


def finish_kernel(mixed, stats, mixed_other, stats_other, out):
    heads, rows = out.shape[3] // HD, out.shape[2]
    for i in range(mixed.shape[0]):
        m0, l0 = stats[i, 0:1], stats[i, 1:2]
        m1, l1 = stats_other[i, 0:1], stats_other[i, 1:2]
        m = jnp.maximum(m0, m1)
        a0 = jnp.exp2((m0 - m) * FACTOR)
        a1 = jnp.exp2((m1 - m) * FACTOR)
        total = l0 * a0 + l1 * a1
        both = mixed[i] * (a0 / total) + mixed_other[i].astype(jnp.float32) * (a1 / total)
        qb, h = i // heads, i % heads
        done = both.T.astype(out.dtype)
        for t in range(BS // rows):
            x, y = divmod(qb * (BS // rows) + t, NY)
            out[x, y, :, h * HD : (h + 1) * HD] = done[t * rows : (t + 1) * rows]


def finish(own, other, shape):
    vmem = pl.BlockSpec(memory_space=pltpu.VMEM)
    return pl.pallas_call(
        finish_kernel,
        out_shape=jax.ShapeDtypeStruct(shape, jnp.bfloat16),
        in_specs=[vmem] * 4,
        out_specs=vmem,
        compiler_params=pltpu.CompilerParams(vmem_limit_bytes=16 << 20),
        cost_estimate=pl.CostEstimate(flops=2000000000, bytes_accessed=4 << 20, transcendentals=1 << 10),
        name="finish",
    )(*own, *other)


def after(x, *behind):
    return lax.optimization_barrier((x,) + behind)[0] if behind else x


def over_x(a):
    return lax.ppermute(a, "head", [(h, (h + NY) % (2 * NY)) for h in range(2 * NY)])


def over_dp(a):
    return lax.ppermute(a, "dp", [(0, 1), (1, 0)])


def project(attended, weights, head, core):
    x, y = head // NY, head % NY

    def at(a, i):
        return lax.dynamic_index_in_dim(a, i % NY, 0, False)

    give = lax.dynamic_index_in_dim(attended, 1 - x, 0, False)
    keep = lax.dynamic_index_in_dim(attended, x, 0, False)
    order = (y - 1, y + 1, y + 2, y)
    got = [over_x(jnp.concatenate([at(give, i) for i in pair])) for pair in (order[:2], order[2:])]
    local = jnp.concatenate([at(keep, i) for i in order])

    rows = got[0].shape[0]
    base = [jnp.dot(local, pair[0], preferred_element_type=jnp.float32) for pair in weights]

    def terms(n, acts, half):
        part = jnp.dot(acts, weights[half][1], preferred_element_type=jnp.float32)
        return jnp.split(part + base[half][n * rows : (n + 1) * rows], 2)

    def narrow(a):
        return a.astype(jnp.bfloat16)

    def turn(a, way):
        to = [(h, h // NY * NY + (h % NY + way) % NY) for h in range(2 * NY)]
        return lax.ppermute(a, "head", to).astype(jnp.float32)

    before, ahead = terms(0, got[0], 0)
    before_down, ahead_down = terms(0, got[0], 1)
    up, down, late = lax.optimization_barrier((narrow(before), narrow(ahead_down), got[1]))
    over, own = terms(1, late, 0)
    over_down, own_down = terms(1, late, 1)
    up = narrow(turn(up, 1) + over)
    down = narrow(turn(down, -1) + over_down)
    for here, here_down in ((ahead, before_down), (own, own_down)):
        up = narrow(turn(up, 1) + here)
        down = narrow(turn(down, -1) + here_down)
    return jnp.where(core == 0, jnp.concatenate([up, down], axis=1), jnp.concatenate([down, up], axis=1))


def on_device(queries, keys, values, block_list, block_count, out_weight):
    rows, width = queries.shape
    per = rows // BS
    blk, head, core = lax.axis_index("blk"), lax.axis_index("head"), lax.axis_index("dp")
    z, xh = blk // NX, blk % NX
    cross = [(b, b ^ 1) for b in range(NZ * NX)]
    up = [(b, (b + NX) % (NZ * NX)) for b in range(NZ * NX)]
    down = [(b, a) for a, b in up]

    asked = lax.ppermute(jnp.concatenate([block_list, block_count[:, None]], axis=1), "blk", cross)
    both = jnp.concatenate([queries, lax.ppermute(queries, "blk", cross)])
    table = jnp.stack([jnp.concatenate([block_list, block_count[:, None]], axis=1), asked])
    listed = jnp.arange(KB, dtype=jnp.int32) < table[..., KB:]
    seen = jnp.any(
        listed[..., None] & (table[..., :KB, None] == jnp.arange(NZ * NX * per, dtype=jnp.int32)), axis=2
    ).astype(jnp.int32)
    seen = lax.dynamic_index_in_dim(seen.reshape(2 * per, NZ, NX, per), xh, 2, False)
    flags = jnp.transpose(seen, (1, 0, 2))[(z - jnp.arange(NZ)) % NZ]

    def visit(stage, state, part=None):
        return attend(
            jnp.stack([flags[d] for d, _, _ in stage]),
            both,
            [k for _, k, _ in stage],
            [v for _, _, v in stage],
            state,
            part,
        )

    stage = ((0, keys, values),)
    state = None
    ups, downs = (keys, values), (keys, values)
    for s in range(1, NZ // 2 + 1):
        if s < NZ // 2:
            ups = tuple(lax.ppermute(a, "blk", up) for a in ups)
            downs = tuple(lax.ppermute(a, "blk", down) for a in downs)
            coming = ((s, *ups), (NZ - s, *downs))
        else:
            coming = ((s, lax.ppermute(ups[0], "blk", up), lax.ppermute(downs[1], "blk", down)),)
        if s == 1:
            half = out_weight.shape[1] // 2
            held = after(out_weight, ups[0])
            ours = lax.dynamic_slice_in_dim(held, core * half, half, 1)
            rest = lax.dynamic_slice_in_dim(held, (1 - core) * half, half, 1)
            fetched = over_x(ours)
        state = visit(stage, state)
        if s < NZ // 2:
            ups = tuple(after(a, state[1]) for a in ups)
            downs = tuple(after(a, state[1]) for a in downs)
        stage = coming
    theirs = visit(stage, state, 1)
    other = [lax.ppermute(a, "blk", cross) for a in theirs]
    mine = visit(stage, (state[0], after(state[1], theirs[1])), 0)
    swapped = over_dp(after(fetched, theirs[1]))
    attended = finish(mine, other, (2, NY, rows // (2 * NY), width))
    return project(attended, ((ours, fetched), (rest, swapped)), head, core)


def solution(mesh):
    placed = (
        P(("dp", "blk"), "head"),
        P(("dp", "blk"), "head"),
        P(("dp", "blk"), "head"),
        P(("dp", "blk"), None),
        P(("dp", "blk")),
        P("head", None),
    )
    return jax.shard_map(
        on_device,
        mesh=mesh,
        in_specs=placed,
        out_specs=P(("dp", "blk", "head"), None),
        check_vma=False,
    )
```

```python
import functools
import math

import jax
import jax.numpy as jnp
from jax import lax
from jax.experimental import pallas as pl
from jax.experimental.pallas import tpu as pltpu
from jax.sharding import PartitionSpec as P

HD = 128
BS = 128
KB = 16
TAB = 16
NZ = 8
NX = 2
NY = 4
LOW = -1e30
FACTOR = math.log2(math.e) / math.sqrt(HD)


def attend_kernel(chunks, first, last, base, flags, q, *refs):
    keys, values = ((refs[0],), (refs[1],)) if chunks == 1 else ((refs[0], refs[3]), (refs[2], refs[1]))
    refs = refs[2 * chunks :]
    heads = q.shape[1] // HD
    per = keys[0].shape[0] // BS
    if first:
        mixed, stats = refs
    else:
        mixed_in, stats_in, mixed, stats = refs[:4]
    acc = refs[4] if last else mixed
    tiles = acc.shape[0]
    if first:
        acc[...] = jnp.zeros_like(acc)
        row = lax.broadcasted_iota(jnp.int32, stats.shape, 1)
        stats[...] = jnp.where(row == 0, LOW, 0.0)
    else:
        acc[...] = mixed_in[base : base + tiles]
        stats[...] = stats_in[base : base + tiles]

    def visit(qb, c, j):
        at = pl.ds(pl.multiple_of(j * BS, BS), BS)
        rows = pl.ds(pl.multiple_of((qb + base // heads) * BS, BS), BS)
        cols = [slice(h * HD, (h + 1) * HD) for h in range(heads)]
        before = [stats[qb * heads + h] for h in range(heads)]
        held = [acc[qb * heads + h] for h in range(heads)]
        scores = [
            lax.dot_general(
                keys[c][at, col], q[rows, col], (((1,), (1,)), ((), ())), preferred_element_type=jnp.float32
            )
            for col in cols
        ]
        after_it = []
        for h in range(heads):
            old, tot = before[h][0:1], before[h][1:2]
            new = jnp.maximum(old, jnp.max(scores[h], axis=0, keepdims=True))
            p = jnp.exp2((scores[h] - new) * FACTOR)
            scale = jnp.exp2((old - new) * FACTOR)
            tot = tot * scale + jnp.sum(p, axis=0, keepdims=True)
            add = lax.dot_general(
                values[c][at, cols[h]],
                p.astype(jnp.bfloat16),
                (((0,), (0,)), ((), ())),
                preferred_element_type=jnp.float32,
            )
            after_it.append((new, tot, held[h] * scale + add))
        for h in range(heads):
            new, tot, total = after_it[h]
            stats[qb * heads + h, 0:1] = new
            stats[qb * heads + h, 1:2] = tot
            acc[qb * heads + h] = total

    def step(n, carry):
        qb, j = n // per, n % per
        for c in range(chunks):

            @pl.when(flags[c, qb + base // heads, j] > 0)
            def _():
                visit(qb, c, j)

        return carry

    lax.fori_loop(0, tiles // heads * per, step, 0)
    if last and base:
        mixed[...] = acc[...].astype(mixed.dtype)
    elif last:
        mixed[...] = acc[...]


def attend(flags, q, keys, values, state, part):
    vmem = pl.BlockSpec(memory_space=pltpu.VMEM)
    smem = pl.BlockSpec(memory_space=pltpu.SMEM)
    last = part is not None
    tiles = q.shape[0] // BS * (q.shape[1] // HD) // (2 if last else 1)
    chunks = len(keys)
    first = state is None
    state = () if first else state
    at = 2 + 2 * chunks
    shape = (tiles, HD, BS)
    return pl.pallas_call(
        functools.partial(attend_kernel, chunks, first, last, tiles * (part or 0)),
        out_shape=(
            jax.ShapeDtypeStruct(shape, jnp.bfloat16 if part else jnp.float32),
            jax.ShapeDtypeStruct((tiles, 8, BS), jnp.float32),
        ),
        in_specs=[smem] + [vmem] * (1 + 2 * chunks + len(state)),
        out_specs=(vmem, vmem),
        input_output_aliases={} if first or last else {at: 0, at + 1: 1},
        scratch_shapes=[pltpu.VMEM(shape, jnp.float32)] if last else [],
        compiler_params=pltpu.CompilerParams(vmem_limit_bytes=24 << 20),
        cost_estimate=pl.CostEstimate(
            flops=tiles * chunks * 100000000, bytes_accessed=4 << 20, transcendentals=chunks << 20
        ),
        name="attend",
    )(flags, q, keys[0], *values[::-1], *keys[1:], *state)


def finish_kernel(mixed, stats, mixed_other, stats_other, out):
    heads, rows = out.shape[3] // HD, out.shape[2]
    for i in range(mixed.shape[0]):
        m0, l0 = stats[i, 0:1], stats[i, 1:2]
        m1, l1 = stats_other[i, 0:1], stats_other[i, 1:2]
        m = jnp.maximum(m0, m1)
        a0 = jnp.exp2((m0 - m) * FACTOR)
        a1 = jnp.exp2((m1 - m) * FACTOR)
        total = l0 * a0 + l1 * a1
        both = mixed[i] * (a0 / total) + mixed_other[i].astype(jnp.float32) * (a1 / total)
        qb, h = i // heads, i % heads
        done = both.T.astype(out.dtype)
        for t in range(BS // rows):
            x, y = divmod(qb * (BS // rows) + t, NY)
            out[x, y, :, h * HD : (h + 1) * HD] = done[t * rows : (t + 1) * rows]


def finish(own, other, shape):
    vmem = pl.BlockSpec(memory_space=pltpu.VMEM)
    return pl.pallas_call(
        finish_kernel,
        out_shape=jax.ShapeDtypeStruct(shape, jnp.bfloat16),
        in_specs=[vmem] * 4,
        out_specs=vmem,
        compiler_params=pltpu.CompilerParams(vmem_limit_bytes=16 << 20),
        cost_estimate=pl.CostEstimate(flops=2000000000, bytes_accessed=4 << 20, transcendentals=1 << 10),
        name="finish",
    )(*own, *other)


def after(x, *behind):
    return lax.optimization_barrier((x,) + behind)[0] if behind else x


def over_x(a):
    return lax.ppermute(a, "head", [(h, (h + NY) % (2 * NY)) for h in range(2 * NY)])


def over_dp(a):
    return lax.ppermute(a, "dp", [(0, 1), (1, 0)])


def project(attended, weights, head, core):
    x, y = head // NY, head % NY

    def at(a, i):
        return lax.dynamic_index_in_dim(a, i % NY, 0, False)

    give = lax.dynamic_index_in_dim(attended, 1 - x, 0, False)
    keep = lax.dynamic_index_in_dim(attended, x, 0, False)
    order = (y - 1, y + 1, y + 2, y)
    got = [over_x(jnp.concatenate([at(give, i) for i in pair])) for pair in (order[:2], order[2:])]
    local = jnp.concatenate([at(keep, i) for i in order])

    rows = got[0].shape[0]
    base = [jnp.dot(local, pair[0], preferred_element_type=jnp.float32) for pair in weights]

    def terms(n, acts, half):
        part = jnp.dot(acts, weights[half][1], preferred_element_type=jnp.float32)
        return jnp.split(part + base[half][n * rows : (n + 1) * rows], 2)

    def narrow(a):
        return a.astype(jnp.bfloat16)

    def turn(a, way):
        to = [(h, h // NY * NY + (h % NY + way) % NY) for h in range(2 * NY)]
        return lax.ppermute(a, "head", to).astype(jnp.float32)

    before, ahead = terms(0, got[0], 0)
    before_down, ahead_down = terms(0, got[0], 1)
    up, down, late = lax.optimization_barrier((narrow(before), narrow(ahead_down), got[1]))
    over, own = terms(1, late, 0)
    over_down, own_down = terms(1, late, 1)
    up = narrow(turn(up, 1) + over)
    down = narrow(turn(down, -1) + over_down)
    for here, here_down in ((ahead, before_down), (own, own_down)):
        up = narrow(turn(up, 1) + here)
        down = narrow(turn(down, -1) + here_down)
    return jnp.where(core == 0, jnp.concatenate([up, down], axis=1), jnp.concatenate([down, up], axis=1))


def on_device(queries, keys, values, block_list, block_count, out_weight):
    rows, width = queries.shape
    per = rows // BS
    blk, head, core = lax.axis_index("blk"), lax.axis_index("head"), lax.axis_index("dp")
    z, xh = blk // NX, blk % NX
    cross = [(b, b ^ 1) for b in range(NZ * NX)]
    up = [(b, (b + NX) % (NZ * NX)) for b in range(NZ * NX)]
    down = [(b, a) for a, b in up]

    asked = lax.ppermute(jnp.concatenate([block_list, block_count[:, None]], axis=1), "blk", cross)
    both = jnp.concatenate([queries, lax.ppermute(queries, "blk", cross)])
    table = jnp.stack([jnp.concatenate([block_list, block_count[:, None]], axis=1), asked])
    listed = jnp.arange(KB, dtype=jnp.int32) < table[..., KB:]
    seen = jnp.any(
        listed[..., None] & (table[..., :KB, None] == jnp.arange(NZ * NX * per, dtype=jnp.int32)), axis=2
    ).astype(jnp.int32)
    seen = lax.dynamic_index_in_dim(seen.reshape(2 * per, NZ, NX, per), xh, 2, False)
    flags = jnp.transpose(seen, (1, 0, 2))[(z - jnp.arange(NZ)) % NZ]

    def visit(stage, state, part=None):
        return attend(
            jnp.stack([flags[d] for d, _, _ in stage]),
            both,
            [k for _, k, _ in stage],
            [v for _, _, v in stage],
            state,
            part,
        )

    stage = ((0, keys, values),)
    state = None
    ups, downs = (keys, values), (keys, values)
    for s in range(1, NZ // 2 + 1):
        if s < NZ // 2:
            key_up, value_down = lax.ppermute(ups[0], "blk", up), lax.ppermute(downs[1], "blk", down)
            ups = key_up, lax.ppermute(ups[1], "blk", up)
            downs = lax.ppermute(downs[0], "blk", down), value_down
            coming = ((s, *ups), (NZ - s, *downs))
        else:
            coming = ((s, lax.ppermute(ups[0], "blk", up), lax.ppermute(downs[1], "blk", down)),)
        if s == 1:
            half = out_weight.shape[1] // 2
            held = after(out_weight, ups[0])
            ours = lax.dynamic_slice_in_dim(held, core * half, half, 1)
            rest = lax.dynamic_slice_in_dim(held, (1 - core) * half, half, 1)
            fetched = over_x(ours)
        state = visit(stage, state)
        if 1 < s < NZ // 2:
            ups = tuple(after(a, state[1]) for a in ups)
            downs = tuple(after(a, state[1]) for a in downs)
        stage = coming
    theirs = visit(stage, state, 1)
    other = [lax.ppermute(a, "blk", cross) for a in theirs]
    mine = visit(stage, (state[0], after(state[1], theirs[1])), 0)
    swapped = over_dp(after(fetched, theirs[1]))
    attended = finish(mine, other, (2, NY, rows // (2 * NY), width))
    return project(attended, ((ours, fetched), (rest, swapped)), head, core)


def solution(mesh):
    placed = (
        P(("dp", "blk"), "head"),
        P(("dp", "blk"), "head"),
        P(("dp", "blk"), "head"),
        P(("dp", "blk"), None),
        P(("dp", "blk")),
        P("head", None),
    )
    return jax.shard_map(
        on_device,
        mesh=mesh,
        in_specs=placed,
        out_specs=P(("dp", "blk", "head"), None),
        check_vma=False,
    )
```

```python
import functools
import math

import jax
import jax.numpy as jnp
from jax import lax
from jax.experimental import pallas as pl
from jax.experimental.pallas import tpu as pltpu
from jax.sharding import PartitionSpec as P

HD = 128
BS = 128
KB = 16
TAB = 16
NZ = 8
NX = 2
NY = 4
LOW = -1e30
FACTOR = math.log2(math.e) / math.sqrt(HD)


def attend_kernel(chunks, first, last, base, flags, q, *refs):
    keys, values = ((refs[0],), (refs[1],)) if chunks == 1 else ((refs[0], refs[3]), (refs[2], refs[1]))
    refs = refs[2 * chunks :]
    heads = q.shape[1] // HD
    per = keys[0].shape[0] // BS
    if first:
        mixed, stats = refs
    else:
        mixed_in, stats_in, mixed, stats = refs[:4]
    acc = refs[4] if last else mixed
    tiles = acc.shape[0]
    if first:
        acc[...] = jnp.zeros_like(acc)
        row = lax.broadcasted_iota(jnp.int32, stats.shape, 1)
        stats[...] = jnp.where(row == 0, LOW, 0.0)
    else:
        acc[...] = mixed_in[base : base + tiles]
        stats[...] = stats_in[base : base + tiles]

    def visit(qb, c, j):
        at = pl.ds(pl.multiple_of(j * BS, BS), BS)
        rows = pl.ds(pl.multiple_of((qb + base // heads) * BS, BS), BS)
        cols = [slice(h * HD, (h + 1) * HD) for h in range(heads)]
        before = [stats[qb * heads + h] for h in range(heads)]
        held = [acc[qb * heads + h] for h in range(heads)]
        scores = [
            lax.dot_general(
                keys[c][at, col], q[rows, col], (((1,), (1,)), ((), ())), preferred_element_type=jnp.float32
            )
            for col in cols
        ]
        after_it = []
        for h in range(heads):
            old, tot = before[h][0:1], before[h][1:2]
            new = jnp.maximum(old, jnp.max(scores[h], axis=0, keepdims=True))
            p = jnp.exp2((scores[h] - new) * FACTOR)
            scale = jnp.exp2((old - new) * FACTOR)
            tot = tot * scale + jnp.sum(p, axis=0, keepdims=True)
            add = lax.dot_general(
                values[c][at, cols[h]],
                p.astype(jnp.bfloat16),
                (((0,), (0,)), ((), ())),
                preferred_element_type=jnp.float32,
            )
            after_it.append((new, tot, held[h] * scale + add))
        for h in range(heads):
            new, tot, total = after_it[h]
            stats[qb * heads + h, 0:1] = new
            stats[qb * heads + h, 1:2] = tot
            acc[qb * heads + h] = total

    def step(n, carry):
        qb, j = n // per, n % per
        for c in range(chunks):

            @pl.when(flags[c, qb + base // heads, j] > 0)
            def _():
                visit(qb, c, j)

        return carry

    lax.fori_loop(0, tiles // heads * per, step, 0)
    if last and base:
        mixed[...] = acc[...].astype(mixed.dtype)
    elif last:
        mixed[...] = acc[...]


def attend(flags, q, keys, values, state, part):
    vmem = pl.BlockSpec(memory_space=pltpu.VMEM)
    smem = pl.BlockSpec(memory_space=pltpu.SMEM)
    last = part is not None
    tiles = q.shape[0] // BS * (q.shape[1] // HD) // (2 if last else 1)
    chunks = len(keys)
    first = state is None
    state = () if first else state
    at = 2 + 2 * chunks
    shape = (tiles, HD, BS)
    return pl.pallas_call(
        functools.partial(attend_kernel, chunks, first, last, tiles * (part or 0)),
        out_shape=(
            jax.ShapeDtypeStruct(shape, jnp.bfloat16 if part else jnp.float32),
            jax.ShapeDtypeStruct((tiles, 8, BS), jnp.float32),
        ),
        in_specs=[smem] + [vmem] * (1 + 2 * chunks + len(state)),
        out_specs=(vmem, vmem),
        input_output_aliases={} if first or last else {at: 0, at + 1: 1},
        scratch_shapes=[pltpu.VMEM(shape, jnp.float32)] if last else [],
        compiler_params=pltpu.CompilerParams(vmem_limit_bytes=24 << 20),
        cost_estimate=pl.CostEstimate(
            flops=tiles * chunks * 100000000, bytes_accessed=4 << 20, transcendentals=chunks << 20
        ),
        name="attend",
    )(flags, q, keys[0], *values[::-1], *keys[1:], *state)


def finish_kernel(mixed, stats, mixed_other, stats_other, out):
    heads, rows = out.shape[3] // HD, out.shape[2]
    for i in range(mixed.shape[0]):
        m0, l0 = stats[i, 0:1], stats[i, 1:2]
        m1, l1 = stats_other[i, 0:1], stats_other[i, 1:2]
        m = jnp.maximum(m0, m1)
        a0 = jnp.exp2((m0 - m) * FACTOR)
        a1 = jnp.exp2((m1 - m) * FACTOR)
        total = l0 * a0 + l1 * a1
        both = mixed[i] * (a0 / total) + mixed_other[i].astype(jnp.float32) * (a1 / total)
        qb, h = i // heads, i % heads
        done = both.T.astype(out.dtype)
        for t in range(BS // rows):
            x, y = divmod(qb * (BS // rows) + t, NY)
            out[x, y, :, h * HD : (h + 1) * HD] = done[t * rows : (t + 1) * rows]


def finish(own, other, shape):
    vmem = pl.BlockSpec(memory_space=pltpu.VMEM)
    return pl.pallas_call(
        finish_kernel,
        out_shape=jax.ShapeDtypeStruct(shape, jnp.bfloat16),
        in_specs=[vmem] * 4,
        out_specs=vmem,
        compiler_params=pltpu.CompilerParams(vmem_limit_bytes=16 << 20),
        cost_estimate=pl.CostEstimate(flops=2000000000, bytes_accessed=4 << 20, transcendentals=1 << 10),
        name="finish",
    )(*own, *other)


def after(x, *behind):
    return lax.optimization_barrier((x,) + behind)[0] if behind else x


def over_x(a):
    return lax.ppermute(a, "head", [(h, (h + NY) % (2 * NY)) for h in range(2 * NY)])


def over_dp(a):
    return lax.ppermute(a, "dp", [(0, 1), (1, 0)])


def project(attended, weights, head, core):
    x, y = head // NY, head % NY

    def at(a, i):
        return lax.dynamic_index_in_dim(a, i % NY, 0, False)

    give = lax.dynamic_index_in_dim(attended, 1 - x, 0, False)
    keep = lax.dynamic_index_in_dim(attended, x, 0, False)
    order = (y - 1, y + 1, y + 2, y)
    got = [over_x(jnp.concatenate([at(give, i) for i in pair])) for pair in (order[:2], order[2:])]
    local = jnp.concatenate([at(keep, i) for i in order])

    rows = got[0].shape[0]
    base = [jnp.dot(local, pair[0], preferred_element_type=jnp.float32) for pair in weights]

    def terms(n, acts, half):
        part = jnp.dot(acts, weights[half][1], preferred_element_type=jnp.float32)
        return jnp.split(part + base[half][n * rows : (n + 1) * rows], 2)

    def narrow(a):
        return a.astype(jnp.bfloat16)

    def turn(a, way):
        to = [(h, h // NY * NY + (h % NY + way) % NY) for h in range(2 * NY)]
        return lax.ppermute(a, "head", to).astype(jnp.float32)

    before, ahead = terms(0, got[0], 0)
    before_down, ahead_down = terms(0, got[0], 1)
    up, down, late = lax.optimization_barrier((narrow(before), narrow(ahead_down), got[1]))
    over, own = terms(1, late, 0)
    over_down, own_down = terms(1, late, 1)
    up = narrow(turn(up, 1) + over)
    down = narrow(turn(down, -1) + over_down)
    for here, here_down in ((ahead, before_down), (own, own_down)):
        up = narrow(turn(up, 1) + here)
        down = narrow(turn(down, -1) + here_down)
    return jnp.where(core == 0, jnp.concatenate([up, down], axis=1), jnp.concatenate([down, up], axis=1))


def on_device(queries, keys, values, block_list, block_count, out_weight):
    rows, width = queries.shape
    per = rows // BS
    blk, head, core = lax.axis_index("blk"), lax.axis_index("head"), lax.axis_index("dp")
    z, xh = blk // NX, blk % NX
    cross = [(b, b ^ 1) for b in range(NZ * NX)]
    up = [(b, (b + NX) % (NZ * NX)) for b in range(NZ * NX)]
    down = [(b, a) for a, b in up]

    asked = lax.ppermute(jnp.concatenate([block_list, block_count[:, None]], axis=1), "blk", cross)
    both = jnp.concatenate([queries, lax.ppermute(queries, "blk", cross)])
    table = jnp.stack([jnp.concatenate([block_list, block_count[:, None]], axis=1), asked])
    listed = jnp.arange(KB, dtype=jnp.int32) < table[..., KB:]
    seen = jnp.any(
        listed[..., None] & (table[..., :KB, None] == jnp.arange(NZ * NX * per, dtype=jnp.int32)), axis=2
    ).astype(jnp.int32)
    seen = lax.dynamic_index_in_dim(seen.reshape(2 * per, NZ, NX, per), xh, 2, False)
    flags = jnp.transpose(seen, (1, 0, 2))[(z - jnp.arange(NZ)) % NZ]

    def visit(stage, state, part=None):
        return attend(
            jnp.stack([flags[d] for d, _, _ in stage]),
            both,
            [k for _, k, _ in stage],
            [v for _, _, v in stage],
            state,
            part,
        )

    stage = ((0, keys, values),)
    state = None
    ups, downs = (keys, values), (keys, values)
    for s in range(1, NZ // 2 + 1):
        if s < NZ // 2:
            key_up, value_down = lax.ppermute(ups[0], "blk", up), lax.ppermute(downs[1], "blk", down)
            ups = key_up, lax.ppermute(ups[1], "blk", up)
            downs = lax.ppermute(downs[0], "blk", down), value_down
            coming = ((s, *ups), (NZ - s, *downs))
        else:
            coming = ((s, lax.ppermute(ups[0], "blk", up), lax.ppermute(downs[1], "blk", down)),)
        if s == 1:
            half = out_weight.shape[1] // 2
            held = after(out_weight, ups[0])
            ours = lax.dynamic_slice_in_dim(held, core * half, half, 1)
            rest = lax.dynamic_slice_in_dim(held, (1 - core) * half, half, 1)
            fetched = over_x(ours)
        state = visit(stage, state)
        if 1 < s < NZ // 2:
            ups = tuple(after(a, state[1]) for a in ups)
            downs = tuple(after(a, state[1]) for a in downs)
        stage = coming
    theirs = visit(stage, state, 1)
    other = [lax.ppermute(a, "blk", cross) for a in theirs]
    mine = visit(stage, (state[0], after(state[1], theirs[1])), 0)
    swapped = over_dp(after(fetched, other[0]))
    attended = finish(mine, other, (2, NY, rows // (2 * NY), width))
    return project(attended, ((ours, fetched), (rest, swapped)), head, core)


def solution(mesh):
    placed = (
        P(("dp", "blk"), "head"),
        P(("dp", "blk"), "head"),
        P(("dp", "blk"), "head"),
        P(("dp", "blk"), None),
        P(("dp", "blk")),
        P("head", None),
    )
    return jax.shard_map(
        on_device,
        mesh=mesh,
        in_specs=placed,
        out_specs=P(("dp", "blk", "head"), None),
        check_vma=False,
    )
```
